256 devices in a mesh: req: 8 (over z), row: 8 (over x, core), col: 4 (over y).
Axes of the slice: x: 4, y: 4, z: 8, core: 2. Of those that a mesh axis runs over, the one named last changes fastest.
Arguments:
- hidden: bfloat16 [4096, 2048], P('req'), as said below
- attention_gain: float32 [2048], replicated, may hold values from 0.5 to 2
- query_weight: bfloat16 [2048, 2048], P('row', 'col'), may hold values from -0.125 to 0.125
- key_value_weight: bfloat16 [2048, 4, 128], P('row', 'col'), may hold values from -0.125 to 0.125
- output_weight: bfloat16 [2048, 2048], P('col', 'row'), may hold values from -0.75 to 0.75
- final_gain: float32 [2048], replicated, may hold values from 0.5 to 2
- head_weight: bfloat16 [2048, 32064], P(None, ('row', 'col')), as said below
- key_value_cache: bfloat16 [64, 2048, 4, 128], P(('req', 'row'), None, 'col'), as said below
- parents: int32 [64, 64], P('req'), may hold values from 0 to 62, as said below
- counts: int32 [64], P('req'), may hold values from 32 to 64, as said below
- lengths: int32 [64], P('req'), may hold values from 1 to 32768
- tokens: int32 [64, 64], P('req'), may hold values from 0 to 32063
- accepted_path: int32 [64, 8], P('req'), may hold values from 0 to 28, as said below
- accept_count: int32 [64], P('req'), may hold values from 1 to 8
Outputs:
- node_logprob: float32 [64, 64], P('req')
- next_logprob: float32 [64, 32064], P('req', ('row', 'col'))
- accepted_cache: bfloat16 [64, 8, 4, 128], P(('req', 'row'), None, 'col')
The draws below stay inside these ranges and needn't reach their ends.
Inputs may be any that keep to these rules, and one draw needn't show every extreme that they name: `hidden`: real values. `head_weight`: real values. `key_value_cache`: real values; slots that the lengths leave empty hold values that must not be used. `parents`: for node i >= 1 the parent is below i and at least i - 4; the entry of node 0 is 0. Nodes 0 to counts[b] - 1 of request b are live, and every ancestor of a live node is live. accepted_path[b, 0] = 0, each entry below accept_count[b] is a live child of the one before, and the entries from accept_count[b] on are 0.
All inputs are finite; a program needn't handle non-finite values.
Results may differ from the reference program's by a relative error of at most 0.0093.
Values may be sent and summed in bfloat16 or wider, within the bound.
A program may use at most 64 MiB of HBM per device.

```python
import math
import jax
import jax.numpy as jnp
import numpy as np
from jax import lax

D = 2048
HEADS = 32
KVH = 4
HD = 64
VOCAB = 32064
WIN = 2048
NODES = 64
PATH = 8
CACHE_MAX = 32768
REQ = 64
TOKENS = 4096


def tree_parts(key):
    node_ids = jnp.arange(NODES, dtype=jnp.int32)
    back_steps = jax.random.randint(jax.random.fold_in(key, 11), (REQ, NODES), 0, 4)
    parents = jnp.maximum(node_ids[None, :] - 1 - back_steps, 0)
    parents = parents.at[:, NODES - 1].set(NODES - 2)
    chain_ids = 4 * jnp.arange(1, PATH, dtype=jnp.int32)
    parents = parents.at[0, chain_ids].set(chain_ids - 4)
    counts = jax.random.randint(jax.random.fold_in(key, 12), (REQ,), NODES // 2, NODES + 1)
    counts = counts.at[0].set(NODES)

    def deepen(index, depths):
        parent_col = parents[:, index]
        parent_depth = jnp.take_along_axis(depths, parent_col[:, None], axis=1)[:, 0]
        return depths.at[:, index].set(jnp.where(index > 0, parent_depth + 1, 0))
    depths = lax.fori_loop(0, NODES, deepen, jnp.zeros((REQ, NODES), jnp.int32))
    end_nodes = (counts - 1).at[0].set(4 * (PATH - 1))
    end_depth = jnp.take_along_axis(depths, end_nodes[:, None], axis=1)[:, 0]
    wanted = jax.random.randint(jax.random.fold_in(key, 13), (REQ,), 1, PATH + 1)
    wanted = wanted.at[0].set(PATH)
    accept = jnp.minimum(end_depth + 1, wanted)
    step_ids = jnp.arange(PATH, dtype=jnp.int32)

    def climb_up(index, carry):
        current, chosen_path = carry
        level_now = jnp.take_along_axis(depths, current[:, None], axis=1)[:, 0]
        chosen_path = jnp.where(step_ids[None, :] == level_now[:, None], current[:, None], chosen_path)
        return (jnp.take_along_axis(parents, current[:, None], axis=1)[:, 0], chosen_path)
    current, chosen_path = lax.fori_loop(0, NODES, climb_up, (end_nodes, jnp.zeros((REQ, PATH), jnp.int32)))
    chosen_path = jnp.where(step_ids[None, :] < accept[:, None], chosen_path, 0)
    return (parents, counts, chosen_path, accept)


def draw_parents(key, part):
    return tree_parts(key)[0]


def draw_counts(key, part):
    return tree_parts(key)[1]


def draw_accepted_path(key, part):
    return tree_parts(key)[2]


def draw_accept_count(key, part):
    return tree_parts(key)[3]


def draw_lengths(key, part):
    powers = jax.random.randint(jax.random.fold_in(key, 21), (REQ,), 0, CACHE_MAX.bit_length() - 1)
    base_length = jnp.left_shift(jnp.ones((REQ,), jnp.int32), powers)
    extra = jax.random.randint(jax.random.fold_in(key, 22), (REQ,), 0, base_length)
    lengths = jnp.minimum(base_length + extra, CACHE_MAX)
    return lengths.at[0].set(CACHE_MAX)


def draw_hidden(key, part):
    row_scale = jnp.exp(jax.random.uniform(jax.random.fold_in(key, 31), (TOKENS, 1), minval=math.log(0.3), maxval=math.log(3.0)))
    column_scale = jnp.exp(jax.random.uniform(jax.random.fold_in(key, 32), (1, D), minval=math.log(0.5), maxval=math.log(2.0)))
    base_values = jnp.clip(jax.random.normal(jax.random.fold_in(key, 33), (TOKENS, D)), -6.0, 6.0)
    return (base_values * row_scale * column_scale).astype(jnp.bfloat16)


def draw_head_weight(key, part):
    values = jnp.clip(jax.random.normal(jax.random.fold_in(key, 41), (D, VOCAB)), -6.0, 6.0) * (3.0 / math.sqrt(D))
    return values.astype(jnp.bfloat16)


def draw_key_value_cache(key, part):
    cache_shape = (REQ, WIN, KVH, 2 * HD)
    values = jnp.clip(jax.random.normal(jax.random.fold_in(key, 51), cache_shape), -6.0, 6.0)
    return values.astype(jnp.bfloat16)


def with_ends(array, stream_key, smallest, top_value):
    shape = array.shape
    place = [jax.random.randint(jax.random.fold_in(stream_key, axis), (), 0, shape[axis]) for axis in range(len(shape))]
    array = array.at[tuple(place)].set(smallest)
    longest = shape.index(max(shape))
    place[longest] = (place[longest] + 1) % shape[longest]
    return array.at[tuple(place)].set(top_value)


def steps_of(own_key, extent, cuts, smallest, largest):
    factor_of = 1.0
    for axis_at, blocks in cuts:
        draws = jax.random.uniform(jax.random.fold_in(jax.random.fold_in(own_key, 6), axis_at), (blocks,), jnp.float32, smallest / len(cuts), largest / len(cuts))
        factor_of = factor_of * jnp.repeat(jnp.exp(draws), extent[axis_at] // blocks).reshape((-1,) + (1,) * (len(extent) - 1 - axis_at))
    return factor_of


def rank_table(count, lean):
    weights = [(1 << 20) // math.isqrt(grade ** lean) + 1 for grade in range(1, count + 1)]
    deviation = 1 + sum(weights) // (1 << 30)
    return np.cumsum(np.array([max(1, weight // deviation) for weight in weights]))


def skewed_ids(stream_key, extent, count, skew):
    grid = rank_table(count, skew)
    pick = jax.random.randint(jax.random.fold_in(stream_key, 1), extent, 0, int(grid[count - 1]))
    rank = jnp.searchsorted(jnp.asarray(grid, jnp.int32), pick, side="right")
    return jax.random.permutation(jax.random.fold_in(stream_key, 2), count)[rank].astype(jnp.int32)


def scatter_about(stream_key, extent, deviation, limit, pieces=(), held_as=jnp.bfloat16):
    entries = deviation * jax.random.normal(stream_key, extent, jnp.float32)
    if pieces:
        entries = entries * steps_of(stream_key, extent, pieces, -0.22, 0.18)
    return jnp.clip(entries, -limit, limit).astype(held_as)


def setup_inputs(seed: int = 0) -> dict:
    keys = jax.random.split(jax.random.key(seed), 15)
    hidden = draw_hidden(jax.random.fold_in(keys[14], 71), 0)
    attention_gain = jnp.clip(jnp.exp(jax.random.uniform(keys[1], (D,), jnp.float32, math.log(0.5), math.log(2.0))), 0.5, 2.0)
    query_weight = scatter_about(keys[2], (D, HEADS * HD), D ** -0.5, 0.125, ((0, 8), (1, 4)))
    key_value_weight = scatter_about(keys[3], (D, KVH, 2 * HD), D ** -0.5, 0.125, ((0, 8), (1, 4)))
    output_weight = scatter_about(keys[4], (HEADS * HD, D), HD ** -0.5, 0.75, ((0, 4), (1, 8)))
    final_gain = jnp.clip(jnp.exp(jax.random.uniform(keys[5], (D,), jnp.float32, math.log(0.5), math.log(2.0))), 0.5, 2.0)
    head_weight = draw_head_weight(jax.random.fold_in(keys[14], 71), 0)
    key_value_cache = draw_key_value_cache(jax.random.fold_in(keys[14], 71), 0)
    parents = draw_parents(jax.random.fold_in(keys[14], 71), 0)
    counts = draw_counts(jax.random.fold_in(keys[14], 71), 0)
    lengths = draw_lengths(jax.random.fold_in(keys[14], 71), 0)
    tokens = with_ends(skewed_ids(keys[11], (REQ, NODES), VOCAB, 2), jax.random.fold_in(keys[11], 3), 0, VOCAB - 1).astype(jnp.int32)
    accepted_path = draw_accepted_path(jax.random.fold_in(keys[14], 71), 0)
    accept_count = draw_accept_count(jax.random.fold_in(keys[14], 71), 0)
    return {"hidden": hidden, "attention_gain": attention_gain, "query_weight": query_weight, "key_value_weight": key_value_weight, "output_weight": output_weight, "final_gain": final_gain, "head_weight": head_weight, "key_value_cache": key_value_cache, "parents": parents, "counts": counts, "lengths": lengths, "tokens": tokens, "accepted_path": accepted_path, "accept_count": accept_count}


epsilon = 1e-05

def ancestry(parents):
    node_count = parents.shape[1]
    node_ids = jnp.arange(node_count, dtype=jnp.int32)
    linked = (parents[:, :, None] == node_ids[None, None, :]) & (node_ids[None, :, None] > 0)
    reached = jnp.eye(node_count, dtype=jnp.float32)[None] + linked.astype(jnp.float32)
    for sweep in range(node_count.bit_length()):
        reached = jnp.minimum(jnp.einsum('bij,bjk->bik', reached, reached, precision=lax.Precision.HIGHEST), 1.0)
    return (reached, lax.optimization_barrier(jnp.sum(reached, axis=2)) - 1.0)

def rotate(values, positions):
    half_size = values.shape[-1] // 2
    frequency = 10000.0 ** (-jnp.arange(half_size, dtype=jnp.float32) / half_size)
    angles = positions[..., None, None] * frequency
    cosine = jnp.cos(angles)
    sine_part = jnp.sin(angles)
    front_half = values[..., :half_size]
    back_half = values[..., half_size:]
    return jnp.concatenate([front_half * cosine - back_half * sine_part, back_half * cosine + front_half * sine_part], axis=-1)

def attend(queries, new_keys, new_values, cache_rows, reached, depths, length):
    node_count, head_count, head_size = queries.shape
    group_count = new_keys.shape[1]
    window_size = cache_rows.shape[0]
    grouped = queries.reshape(node_count, group_count, head_count // group_count, head_size).astype(jnp.float32)
    all_keys = jnp.concatenate([cache_rows[:, :, :head_size], new_keys], axis=0).astype(jnp.float32)
    all_values = jnp.concatenate([cache_rows[:, :, head_size:], new_values], axis=0).astype(jnp.float32)
    scores = jnp.einsum('ngqd,kgd->gqnk', grouped, all_keys) * (1.0 / math.sqrt(head_size))
    slot_ids = jnp.arange(window_size, dtype=jnp.float32)
    cache_open = (slot_ids[None, :] > depths[:, None]) & (slot_ids[None, :] >= (window_size - length).astype(jnp.float32))
    allowed = jnp.concatenate([cache_open, reached > 0.5], axis=1)
    scores = jnp.where(allowed[None, None], scores, -jnp.inf)
    row_max = lax.optimization_barrier(jnp.max(scores, axis=3, keepdims=True))
    weights = jnp.exp(scores - row_max)
    weights_bf = (weights / lax.optimization_barrier(jnp.sum(weights, axis=3, keepdims=True))).astype(jnp.bfloat16)
    attended = jnp.einsum('gqnk,kgd->ngqd', weights_bf.astype(jnp.float32), all_values)
    return attended.reshape(node_count, head_count * head_size).astype(jnp.bfloat16)

def attend_packed(packed):
    return attend(*packed)

def reference(hidden, attention_gain, query_weight, key_value_weight, output_weight, final_gain, head_weight, key_value_cache, parents, counts, lengths, tokens, accepted_path, accept_count):
    requests = parents.shape[0]
    widened = hidden.astype(jnp.float32)
    normed = (widened * lax.rsqrt(lax.optimization_barrier(jnp.mean(widened * widened, axis=1, keepdims=True)) + epsilon) * attention_gain).astype(jnp.bfloat16)
    raw_queries = jnp.dot(normed, query_weight, preferred_element_type=jnp.float32).reshape(requests, NODES, HEADS, HD)
    raw_pairs = jnp.dot(normed, key_value_weight.reshape(D, KVH * 2 * HD), preferred_element_type=jnp.float32).reshape(requests, NODES, KVH, 2 * HD)
    reached, depths = ancestry(parents)
    positions = lengths[:, None].astype(jnp.float32) + depths
    queries = rotate(raw_queries, positions).astype(jnp.bfloat16)
    new_keys = rotate(raw_pairs[..., :HD], positions).astype(jnp.bfloat16)
    new_values = raw_pairs[..., HD:].astype(jnp.bfloat16)
    attended = lax.map(attend_packed, (queries, new_keys, new_values, key_value_cache, reached, depths, lengths))
    attended = attended.reshape(requests * NODES, HEADS * HD)
    residual = widened + jnp.dot(attended, output_weight, preferred_element_type=jnp.float32)
    normed_out = (residual * lax.rsqrt(lax.optimization_barrier(jnp.mean(residual * residual, axis=1, keepdims=True)) + epsilon) * final_gain).astype(jnp.bfloat16)
    node_ids = jnp.arange(NODES, dtype=jnp.int32)
    last_nodes = jnp.take_along_axis(accepted_path, (accept_count - 1)[:, None], axis=1)[:, 0]

    def score_request(packed):
        row_block, chosen, links, live_count, last_node = packed
        logits = jnp.dot(row_block, head_weight, preferred_element_type=jnp.float32)
        row_max = lax.optimization_barrier(jnp.max(logits, axis=1))
        log_total = row_max + jnp.log(lax.optimization_barrier(jnp.sum(jnp.exp(logits - row_max[:, None]), axis=1)))
        picked = logits[links, chosen]
        node_score = jnp.where((node_ids > 0) & (node_ids < live_count), picked - log_total[links], jnp.zeros_like(picked))
        return (node_score, logits[last_node] - log_total[last_node])
    node_logprob, next_logprob = lax.map(score_request, (normed_out.reshape(requests, NODES, D), tokens, parents, counts, last_nodes))
    fresh_rows = jnp.concatenate([new_keys, new_values], axis=3)
    chosen_rows = jnp.take_along_axis(fresh_rows, accepted_path[:, :, None, None], axis=1)
    step_ids = jnp.arange(PATH, dtype=jnp.int32)
    kept_rows = (step_ids[None, :] < accept_count[:, None])[:, :, None, None]
    accepted_cache = jnp.where(kept_rows, chosen_rows, jnp.zeros_like(chosen_rows))
    return (node_logprob, next_logprob, accepted_cache)
```

```python
import functools

import jax
import jax.numpy as jnp
import numpy as np
from jax import lax
from jax.experimental import pallas as pl
from jax.experimental.pallas import tpu as pltpu
from jax.sharding import PartitionSpec as P

D = 2048
NODES = 64
WIN = 2048
VW = 1002
F32 = jnp.float32
BF16 = jnp.bfloat16
EPS = 1e-5
NEAR_FIRST = (1, 3, 2)


def dot(a, b):
    return jnp.dot(a, b, preferred_element_type=F32)


def dot_nt(a, b):
    return lax.dot_general(a, b, (((1,), (1,)), ((), ())), preferred_element_type=F32)


def body(
    hid, again, wq, wkv, wo, fgain, wh, cache, par, tok, path, freq,
    counts, lengths, accepts,
    out_node, out_next, out_cache,
    H, AG, W1, WO, FG, WV, C, PAR, TOK, PATH, FREQ,
    PF, NB, send1, recv1, A, PO, send2, recv2, G, ACC, IG2,
    st1, st2, nx_send, nx_recv,
    lsem, psend, precv, s1s, s1r, as_, ar, s2s, s2r, gas, gar, gbs, gbr,
    t1s, t1r, t2s, t2r, nxs, nxr,
):
    r = lax.axis_index("row")
    y = lax.axis_index("col")
    x = lax.div(r, 2)
    k = lax.rem(r, 2)
    other = 1 - k
    me = r

    def dev(x2, k2, y2):
        return {"row": 2 * x2 + k2, "col": y2}

    def ring(v, d):
        return lax.rem(v + d, 4)

    def remote(src, dst, ssem, rsem, where):
        return pltpu.make_async_remote_copy(
            src_ref=src, dst_ref=dst, send_sem=ssem, recv_sem=rsem,
            device_id=where, device_id_type=pl.DeviceIdType.MESH,
        )

    def rows(i, n=64):
        return pl.ds(pl.multiple_of(i * n, n), n)

    barrier = pltpu.get_barrier_semaphore()
    peers = [dev(x, other, y)]
    for d in (1, 2, 3):
        peers += [dev(ring(x, d), k, y), dev(ring(x, d), other, y), dev(x, k, ring(y, d))]
    for p in peers:
        pl.semaphore_signal(barrier, inc=1, device_id=p, device_id_type=pl.DeviceIdType.MESH)

    local = []

    def fetch(src, dst):
        copy = pltpu.make_async_copy(src, dst, lsem.at[len(local)])
        copy.start()
        local.append(copy)
        return copy

    h_copies = [fetch(hid.at[pl.ds(pl.multiple_of((2 * q + k) * 64, 64), 64)], H.at[pl.ds(64 * q, 64)]) for q in range(4)]
    small = [fetch(a, b) for a, b in ((again, AG), (par, PAR), (path, PATH), (freq, FREQ))]
    half_rows = rows(k, 256)
    w1_copies = [fetch(wq, W1.at[half_rows, pl.ds(0, 512)]), fetch(wkv, W1.at[half_rows, pl.ds(512, 128)])]
    c_copy = fetch(cache, C)
    late = [fetch(fgain, FG), fetch(tok, TOK)]
    wo_copy = fetch(wo, WO.at[:, half_rows])
    wh_copies = []
    for xx in range(4):
        for h in range(2):
            wh_copies.append(fetch(wh.at[:, pl.ds(512 * xx + 256 * h, 256)], WV.at[0, h, :, pl.ds(256 * xx, 256)]))

    pl.semaphore_wait(barrier, len(peers))

    partner = dev(x, other, y)
    swaps = []

    def swap(src, dst):
        copy = remote(src, dst, psend.at[len(swaps)], precv.at[len(swaps)], partner)
        copy.start()
        swaps.append(copy)
        return copy

    w1_swaps = [swap(wq, W1.at[half_rows, pl.ds(0, 512)]), swap(wkv, W1.at[half_rows, pl.ds(512, 128)])]
    wo_swap = swap(wo, WO.at[:, half_rows])
    wh_swaps = []
    for xx in range(4):
        for h in range(2):
            wh_swaps.append(swap(wh.at[:, pl.ds(512 * xx + 256 * h, 256)], WV.at[1, h, :, pl.ds(256 * xx, 256)]))

    for c in small:
        c.wait()
    own_cols = pl.ds(pl.multiple_of(512 * x, 512), 512)
    gain_row = AG[:, own_cols]
    for q in range(4):
        h_copies[q].wait()
        wide = H[pl.ds(64 * q, 64), :].astype(F32)
        inv = lax.rsqrt(jnp.sum(wide * wide, axis=1, keepdims=True) * (1.0 / D) + EPS)
        part = H[pl.ds(64 * q, 64), own_cols].astype(F32)
        NB[pl.ds(64 * q, 64), :] = (part * inv * gain_row).astype(BF16)
    for c in w1_copies:
        c.wait()
    for c in w1_swaps:
        c.wait_recv()
    PF[...] = dot(NB[...], W1[...])
    first = []
    for d in NEAR_FIRST:
        q = ring(x, d)
        send1[d] = PF[rows(q), :].astype(BF16)
        copy = remote(send1.at[d], recv1.at[d], s1s.at[d], s1r.at[d], dev(q, k, y))
        copy.start()
        first.append(copy)

    lane64 = lax.broadcasted_iota(jnp.int32, (64, 64), 1)
    sub64 = lax.broadcasted_iota(jnp.int32, (64, 64), 0)
    eye = lane64 == sub64
    eye8 = lax.broadcasted_iota(jnp.int32, (8, 8), 0) == lax.broadcasted_iota(jnp.int32, (8, 8), 1)

    def column(row_values):
        return jnp.sum(jnp.where(eye, row_values, 0), axis=1, keepdims=True)

    def parent_column(b):
        return column(PAR[pl.ds(b, 1), :])

    def gather_matrix(b, parents_col):
        path_row = PATH[pl.ds(b, 1), :]
        lane8 = lax.broadcasted_iota(jnp.int32, (1, 8), 1)
        last = jnp.sum(jnp.where(lane8 == accepts[b] - 1, path_row, 0), axis=1, keepdims=True)
        source = jnp.where(sub64[:, :1] == 0, last, parents_col)
        return jnp.where(source == lane64, 1.0, 0.0).astype(BF16)

    parents_col = parent_column(me)
    reach = jnp.where(eye | ((parents_col == lane64) & (sub64 > 0)), 1.0, 0.0)
    for _ in range(6):
        half = reach.astype(BF16)
        reach = jnp.minimum(dot(half, half), 1.0)
    depth = jnp.sum(reach, axis=1, keepdims=True) - 1.0
    length = lengths[me]
    angles = (length.astype(F32) + depth) * FREQ[...]
    cosine = jnp.cos(angles)
    sine = jnp.sin(angles)
    closed = jnp.maximum(depth.astype(jnp.int32), WIN - 1 - length)
    gather_own = gather_matrix(me, parents_col)
    gather_y = gather_matrix(2 * y + k, parent_column(2 * y + k))
    hid_y = dot(gather_y, H[rows(y), own_cols])

    lane = lax.broadcasted_iota(jnp.int32, (64, 128), 1)
    front = lax.rem(lane, 64) < 32
    low = lane < 64

    def rotated(u):
        turned = jnp.where(front, -pltpu.roll(u, 96, 1), pltpu.roll(u, 32, 1))
        return u * cosine + turned * sine

    eye256 = lax.broadcasted_iota(jnp.int32, (256, 256), 0) == lax.broadcasted_iota(jnp.int32, (256, 256), 1)

    def as_row(col):
        return jnp.sum(jnp.where(eye256, col, jnp.zeros_like(col)), axis=0, keepdims=True)

    c_copy.wait()
    for c in late:
        c.wait()
    IG2[...] = 1.0 / (FG[...] * FG[...])
    token_cols = [column(TOK[pl.ds(2 * q + k, 1), :]) for q in range(4)]
    token_row = as_row(jnp.concatenate(token_cols, axis=0))

    for copy in first:
        copy.wait_recv()
    raw = PF[rows(x), :] + recv1[1].astype(F32) + recv1[2].astype(F32) + recv1[3].astype(F32)
    pair = raw[:, 512:640]
    fresh = jnp.where(low, rotated(pair), pair).astype(BF16)
    path_row = PATH[pl.ds(me, 1), :]
    path_col = jnp.sum(jnp.where(eye8, path_row, 0), axis=1, keepdims=True)
    lane8x64 = lax.broadcasted_iota(jnp.int32, (8, 64), 1)
    sub8x64 = lax.broadcasted_iota(jnp.int32, (8, 64), 0)
    chosen = jnp.where((path_col == lane8x64) & (sub8x64 < accepts[me]), 1.0, 0.0).astype(BF16)
    out_cache[...] = dot(chosen, fresh).astype(BF16)

    slot = lax.broadcasted_iota(jnp.int32, (256, WIN), 1)
    closed4 = jnp.concatenate([closed] * 4, axis=0)
    reach4 = jnp.concatenate([reach] * 4, axis=0) > 0.5
    spread = []
    for hc in range(2):
        stack = []
        for j in range(2):
            at = 256 * hc + 128 * j
            turned = rotated(raw[:, at : at + 128]).astype(BF16).astype(F32) * 0.125
            stack.append(jnp.where(low, turned, 0.0))
            stack.append(jnp.where(low, pltpu.roll(turned, 64, 1), 0.0))
        queries = jnp.concatenate(stack, axis=0).astype(BF16)
        scores = jnp.where(slot > closed4, dot_nt(queries, C[...]), -jnp.inf)
        scores_new = jnp.where(reach4, dot_nt(queries, fresh), -jnp.inf)
        top = jnp.maximum(jnp.max(scores, axis=1, keepdims=True), jnp.max(scores_new, axis=1, keepdims=True))
        w = jnp.exp(scores - top)
        w_new = jnp.exp(scores_new - top)
        total = jnp.sum(w, axis=1, keepdims=True) + jnp.sum(w_new, axis=1, keepdims=True)
        o = (dot(w.astype(BF16), C[...]) + dot(w_new.astype(BF16), fresh)) / total
        blocks = [
            jnp.where(low, pltpu.roll(o[128 * j : 128 * j + 64], 64, 1), o[128 * j + 64 : 128 * j + 128])
            for j in range(2)
        ]
        attended = jnp.concatenate(blocks, axis=1).astype(BF16)
        A[hc, rows(x), :] = dot(gather_own, attended).astype(BF16)
        for d in NEAR_FIRST:
            at = A.at[hc, rows(x)]
            copy = remote(at, at, as_.at[hc, d], ar.at[hc, d], dev(ring(x, d), k, y))
            copy.start()
            spread.append(copy)

    wo_copy.wait()
    wo_swap.wait_recv()
    for copy in spread:
        copy.wait_recv()
    second = {}
    for h in range(2):
        cols = pl.ds(256 * h, 256)
        PO[h] = dot(A[0], WO[pl.ds(0, 256), cols]) + dot(A[1], WO[pl.ds(256, 256), cols])
        for d in NEAR_FIRST:
            q = ring(y, d)
            send2[h, d] = PO[h, rows(q), :].astype(BF16)
            copy = remote(send2.at[h, d], recv2.at[h, d], s2s.at[h, d], s2r.at[h, d], dev(x, k, q))
            copy.start()
            second[h, d] = copy

    def piece(h, xx, yy):
        return G.at[h, rows(yy), pl.ds(pl.multiple_of(256 * xx, 256), 256)]

    def stage_one_copy(h, d):
        at = piece(h, x, y)
        where = dev(x, k, ring(y, d)) if h == 0 else dev(ring(x, d), k, y)
        return remote(at, at, gas.at[h, d], gar.at[h, d], where)

    def stage_two_copy(h, e, d):
        if h == 0:
            at = piece(0, x, ring(y, 4 - d))
            where = dev(ring(x, e), k, y)
        else:
            at = piece(1, ring(x, 4 - d), y)
            where = dev(x, k, ring(y, e))
        return remote(at, at, gbs.at[h, e, d], gbr.at[h, e, d], where)

    stage_one, stage_two = {}, {}
    for h in range(2):
        for d in NEAR_FIRST:
            second[h, d].wait_recv()
        res = (
            PO[h, rows(y), :]
            + recv2[h, 1].astype(F32) + recv2[h, 2].astype(F32) + recv2[h, 3].astype(F32)
            + hid_y[:, 256 * h : 256 * h + 256]
        )
        gain = FG[:, pl.ds(pl.multiple_of(512 * x + 256 * h, 256), 256)]
        G[h, rows(y), pl.ds(pl.multiple_of(256 * x, 256), 256)] = (res * gain).astype(BF16)
        for d in NEAR_FIRST:
            stage_one[h, d] = stage_one_copy(h, d)
            stage_one[h, d].start()
        for e in NEAR_FIRST:
            stage_two[h, e, 0] = stage_two_copy(h, e, 0)
            stage_two[h, e, 0].start()
    for d in NEAR_FIRST:
        for h in range(2):
            stage_one[h, d].wait_recv()
            for e in NEAR_FIRST:
                stage_two[h, e, d] = stage_two_copy(h, e, d)
                stage_two[h, e, d].start()

    for c in wh_copies:
        c.wait()
    for c in wh_swaps:
        c.wait_recv()

    def squares(h, xx):
        u = G[h, :, pl.ds(pl.multiple_of(256 * xx, 256), 256)].astype(F32)
        scale = IG2[:, pl.ds(pl.multiple_of(512 * xx + 256 * h, 256), 256)]
        return jnp.sum(u * u * scale, axis=1, keepdims=True)

    sq = jnp.zeros((256, 1), F32)
    for e in (0,) + NEAR_FIRST:
        xx = ring(x, 4 - e)
        if e:
            for d in range(4):
                stage_two[0, e, d].wait_recv()
        sq = sq + squares(0, xx)
        cols = rows(xx, 256)
        rhs = G[0, :, cols]

        def add_chunk(s, carry, rhs=rhs, cols=cols, begin=(e == 0)):
            term = dot_nt(WV[s, 0, :, cols], rhs)
            ACC[s] = term if begin else ACC[s] + term
            return carry

        lax.fori_loop(0, 2, add_chunk, 0)
    for e in NEAR_FIRST:
        for d in range(4):
            stage_two[1, e, d].wait_recv()
    for xx in range(4):
        sq = sq + squares(1, xx)
    inv = as_row(lax.rsqrt(sq * (1.0 / D) + EPS))

    def finish(s, top):
        t = (ACC[s] + dot_nt(WV[s, 1], G[1])) * inv
        ACC[s] = t
        return jnp.maximum(top, jnp.max(t, axis=0, keepdims=True))

    top = lax.fori_loop(0, 2, finish, jnp.full((1, 256), -jnp.inf, F32))
    vocab = lax.broadcasted_iota(jnp.int32, (VW, 256), 0)

    def totals(s, carry):
        total, pick = carry
        t = ACC[s]
        holder = jnp.where(s == 0, k, other)
        start = ((2 * x + holder) * 4 + y) * VW
        total = total + jnp.sum(jnp.exp(t - top), axis=0, keepdims=True)
        pick = pick + jnp.sum(jnp.where(vocab == token_row - start, t, 0.0), axis=0, keepdims=True)
        return total, pick

    zero = jnp.zeros((1, 256), F32)
    total, pick = lax.fori_loop(0, 2, totals, (zero, zero))
    st1[0] = jnp.concatenate([top, total, pick, jnp.zeros((5, 256), F32)], axis=0)
    third = []
    for d in NEAR_FIRST:
        copy = remote(st1.at[0], st1.at[d], t1s.at[d], t1r.at[d], dev(x, k, ring(y, d)))
        copy.start()
        third.append(copy)

    first_of = lax.broadcasted_iota(jnp.int32, (8, 256), 0) * 64 == lax.broadcasted_iota(jnp.int32, (8, 256), 1)
    first_of = jnp.where(first_of, 1.0, 0.0)

    def last_rows(s):
        return lax.dot_general(
            first_of, ACC[s], (((1,), (1,)), ((), ())),
            precision=lax.Precision.HIGHEST, preferred_element_type=F32,
        )

    nx_send[...] = last_rows(1)
    nx = remote(nx_send, nx_recv, nxs, nxr, partner)
    nx.start()
    own_next = last_rows(0)

    def combine(parts):
        tops = [p[0:1] for p in parts]
        m = functools.reduce(jnp.maximum, tops)
        total = sum(p[1:2] * jnp.exp(t - m) for p, t in zip(parts, tops))
        pick = sum(p[2:3] for p in parts)
        return m, total, pick

    for copy in third:
        copy.wait_recv()
    m, total4, pick4 = combine([st1[d] for d in range(4)])
    st2[me] = jnp.concatenate([m, total4, pick4, jnp.zeros((5, 256), F32)], axis=0)
    fourth = []
    for i, (d, flip) in enumerate(((0, 1), (1, 0), (1, 1), (3, 0), (3, 1), (2, 0), (2, 1))):
        copy = remote(
            st2.at[me], st2.at[me], t2s.at[i], t2r.at[i],
            dev(ring(x, d), other if flip else k, y),
        )
        copy.start()
        fourth.append(copy)
    nx.wait_recv()
    for copy in fourth:
        copy.wait_recv()
    lane1 = lax.broadcasted_iota(jnp.int32, (1, 64), 1)
    for plane in range(2):
        m, total4, pick4 = combine([st2[2 * xx + plane] for xx in range(4)])
        log_total = m + jnp.log(total4)
        score = pick4 - log_total
        for q in range(4):
            b = 2 * q + plane
            at = slice(64 * q, 64 * q + 64)
            live = (lane1 > 0) & (lane1 < counts[b])
            out_node[pl.ds(b, 1), :] = jnp.where(live, score[:, at], 0.0)
            row = jnp.where(k == plane, own_next[q : q + 1], nx_recv[pl.ds(q, 1), :])
            out_next[pl.ds(b, 1), :] = row - log_total[:, 64 * q : 64 * q + 1]

    for copy in swaps + first + spread + list(second.values()) + list(stage_one.values()):
        copy.wait_send()
    for copy in list(stage_two.values()) + third + fourth + [nx]:
        copy.wait_send()


def shards(
    hidden, attention_gain, query_weight, key_value_weight, output_weight, final_gain, head_weight,
    key_value_cache, parents, counts, lengths, tokens, accepted_path, accept_count,
):
    half = 32
    freq = 10000.0 ** (-np.arange(half, dtype=np.float64) / half)
    freq = jnp.asarray(np.tile(freq, 4)[None], F32)
    anywhere = pl.BlockSpec(memory_space=pl.ANY)
    scalars = pl.BlockSpec(memory_space=pltpu.SMEM)
    vmem = pl.BlockSpec(memory_space=pltpu.VMEM)
    dma = pltpu.SemaphoreType.DMA
    node, following, cache_rows = pl.pallas_call(
        body,
        out_shape=(
            jax.ShapeDtypeStruct((8, NODES), F32),
            jax.ShapeDtypeStruct((8, VW), F32),
            jax.ShapeDtypeStruct((8, 128), BF16),
        ),
        in_specs=[anywhere] * 12 + [scalars] * 3,
        out_specs=(vmem, vmem, vmem),
        scratch_shapes=[
            pltpu.VMEM((256, D), BF16),
            pltpu.VMEM((1, D), F32),
            pltpu.VMEM((512, 640), BF16),
            pltpu.VMEM((512, 512), BF16),
            pltpu.VMEM((1, D), F32),
            pltpu.VMEM((2, 2, VW, 1024), BF16),
            pltpu.VMEM((WIN, 128), BF16),
            pltpu.VMEM((8, NODES), jnp.int32),
            pltpu.VMEM((8, NODES), jnp.int32),
            pltpu.VMEM((8, 8), jnp.int32),
            pltpu.VMEM((1, 128), F32),
            pltpu.VMEM((256, 640), F32),
            pltpu.VMEM((256, 512), BF16),
            pltpu.VMEM((4, 64, 640), BF16),
            pltpu.VMEM((4, 64, 640), BF16),
            pltpu.VMEM((2, 256, 256), BF16),
            pltpu.VMEM((2, 256, 256), F32),
            pltpu.VMEM((2, 4, 64, 256), BF16),
            pltpu.VMEM((2, 4, 64, 256), BF16),
            pltpu.VMEM((2, 256, 1024), BF16),
            pltpu.VMEM((2, VW, 256), F32),
            pltpu.VMEM((1, D), F32),
            pltpu.VMEM((4, 8, 256), F32),
            pltpu.VMEM((8, 8, 256), F32),
            pltpu.VMEM((8, VW), F32),
            pltpu.VMEM((8, VW), F32),
            dma((24,)), dma((12,)), dma((12,)),
            dma((4,)), dma((4,)), dma((2, 4)), dma((2, 4)), dma((2, 4)), dma((2, 4)),
            dma((2, 4)), dma((2, 4)), dma((2, 4, 4)), dma((2, 4, 4)),
            dma((4,)), dma((4,)), dma((8,)), dma((8,)), dma(()), dma(()),
        ],
        compiler_params=pltpu.CompilerParams(
            collective_id=0, has_side_effects=True, vmem_limit_bytes=60 * 1024 * 1024
        ),
        name="verify",
    )(
        hidden,
        attention_gain.reshape(1, D),
        query_weight,
        key_value_weight.reshape(256, 128),
        output_weight,
        final_gain.reshape(1, D),
        head_weight.T,
        key_value_cache.reshape(WIN, 128),
        parents,
        tokens,
        accepted_path,
        freq,
        counts,
        lengths,
        accept_count,
    )
    return node, following, cache_rows.reshape(1, 8, 1, 128)


def solution(mesh):
    in_specs = (
        P("req", None),
        P(),
        P("row", "col"),
        P("row", "col", None),
        P("col", "row"),
        P(),
        P(None, ("row", "col")),
        P(("req", "row"), None, "col", None),
        P("req", None),
        P("req"),
        P("req"),
        P("req", None),
        P("req", None),
        P("req"),
    )
    out_specs = (P("req", None), P("req", ("row", "col")), P(("req", "row"), None, "col", None))
    return jax.shard_map(shards, mesh=mesh, in_specs=in_specs, out_specs=out_specs, check_vma=False)
```

```python
import functools

import jax
import jax.numpy as jnp
import numpy as np
from jax import lax
from jax.experimental import pallas as pl
from jax.experimental.pallas import tpu as pltpu
from jax.sharding import PartitionSpec as P

D = 2048
NODES = 64
WIN = 2048
VW = 1002
F32 = jnp.float32
BF16 = jnp.bfloat16
EPS = 1e-5
NEAR_FIRST = (1, 3, 2)
FAR_FIRST = (2, 1, 3, 0)


def dot(a, b):
    return jnp.dot(a, b, preferred_element_type=F32)


def dot_nt(a, b):
    return lax.dot_general(a, b, (((1,), (1,)), ((), ())), preferred_element_type=F32)


def body(
    hid, again, wq, wkv, wo, fgain, wh, cache, par, tok, path, freq,
    counts, lengths, accepts,
    out_node, out_next, out_cache,
    H, AG, W1, WO, FG, WV, C, PAR, TOK, PATH, FREQ,
    PF, NB, send1, recv1, EQ, AS, AR, G, ACC, IG2, ST, nx_send, nx_recv,
    lsem, psend, precv, wys, wyr, wps, wpr, s1s, s1r, axs, axr,
    gas, gar, gbs, gbr, sts, str_, nxs, nxr,
):
    r = lax.axis_index("row")
    y = lax.axis_index("col")
    x = lax.div(r, 2)
    k = lax.rem(r, 2)
    other = 1 - k
    me = r

    def dev(x2, k2, y2):
        return {"row": 2 * x2 + k2, "col": y2}

    def ring(v, d):
        return lax.rem(v + d, 4)

    def remote(src, dst, ssem, rsem, where):
        return pltpu.make_async_remote_copy(
            src_ref=src, dst_ref=dst, send_sem=ssem, recv_sem=rsem,
            device_id=where, device_id_type=pl.DeviceIdType.MESH,
        )

    def rows(i, n=64):
        return pl.ds(pl.multiple_of(i * n, n), n)

    barrier = pltpu.get_barrier_semaphore()
    everyone = [(dx, dy, flip) for dx in FAR_FIRST for dy in FAR_FIRST for flip in (0, 1) if dx or dy or flip]
    peers = [dev(ring(x, dx), other if flip else k, ring(y, dy)) for dx, dy, flip in everyone]
    for p in peers:
        pl.semaphore_signal(barrier, inc=1, device_id=p, device_id_type=pl.DeviceIdType.MESH)

    local = []

    def fetch(src, dst):
        copy = pltpu.make_async_copy(src, dst, lsem.at[len(local)])
        copy.start()
        local.append(copy)
        return copy

    h_copies = [fetch(hid.at[pl.ds(pl.multiple_of((2 * q + k) * 64, 64), 64)], H.at[pl.ds(64 * q, 64)]) for q in range(4)]
    small = [fetch(a, b) for a, b in ((again, AG), (par, PAR), (path, PATH), (freq, FREQ))]
    half_rows = rows(k, 256)
    w1_copies = [fetch(wq, W1.at[half_rows, pl.ds(0, 512)]), fetch(wkv, W1.at[half_rows, pl.ds(512, 128)])]
    c_copy = fetch(cache, C)
    late = [fetch(fgain, FG), fetch(tok, TOK)]

    def wo_piece(hc, yy):
        return WO.at[hc, rows(yy, 256), half_rows]

    wo_copies = [fetch(wo.at[pl.ds(256 * hc, 256)], wo_piece(hc, y)) for hc in range(2)]
    wh_copies = []
    for xx in range(4):
        for h in range(2):
            wh_copies.append(fetch(wh.at[:, pl.ds(512 * xx + 256 * h, 256)], WV.at[0, h, :, pl.ds(256 * xx, 256)]))

    pl.semaphore_wait(barrier, len(peers))

    partner = dev(x, other, y)
    swaps = []

    def swap(src, dst):
        copy = remote(src, dst, psend.at[len(swaps)], precv.at[len(swaps)], partner)
        copy.start()
        swaps.append(copy)
        return copy

    w1_swaps = [swap(wq, W1.at[half_rows, pl.ds(0, 512)]), swap(wkv, W1.at[half_rows, pl.ds(512, 128)])]
    wo_swaps = [swap(wo.at[pl.ds(256 * hc, 256)], wo_piece(hc, y)) for hc in range(2)]
    wo_gathers = {}
    for d in NEAR_FIRST:
        for hc in range(2):
            copy = remote(wo.at[pl.ds(256 * hc, 256)], wo_piece(hc, y), wys.at[hc, d], wyr.at[hc, d], dev(x, k, ring(y, d)))
            copy.start()
            wo_gathers[hc, d] = copy
    wh_swaps = []
    for xx in range(4):
        for h in range(2):
            wh_swaps.append(swap(wh.at[:, pl.ds(512 * xx + 256 * h, 256)], WV.at[1, h, :, pl.ds(256 * xx, 256)]))

    for c in small:
        c.wait()
    own_cols = pl.ds(pl.multiple_of(512 * x, 512), 512)
    gain_row = AG[:, own_cols]
    for q in range(4):
        h_copies[q].wait()
        wide = H[pl.ds(64 * q, 64), :].astype(F32)
        inv = lax.rsqrt(jnp.sum(wide * wide, axis=1, keepdims=True) * (1.0 / D) + EPS)
        part = H[pl.ds(64 * q, 64), own_cols].astype(F32)
        NB[pl.ds(64 * q, 64), :] = (part * inv * gain_row).astype(BF16)
    for c in w1_copies:
        c.wait()
    for c in w1_swaps:
        c.wait_recv()
    PF[...] = dot(NB[...], W1[...])
    first = []
    for d in NEAR_FIRST:
        q = ring(x, d)
        send1[d] = PF[rows(q), :].astype(BF16)
        copy = remote(send1.at[d], recv1.at[d], s1s.at[d], s1r.at[d], dev(q, k, y))
        copy.start()
        first.append(copy)

    lane64 = lax.broadcasted_iota(jnp.int32, (64, 64), 1)
    sub64 = lax.broadcasted_iota(jnp.int32, (64, 64), 0)
    eye = lane64 == sub64
    eye8 = lax.broadcasted_iota(jnp.int32, (8, 8), 0) == lax.broadcasted_iota(jnp.int32, (8, 8), 1)

    def column(row_values):
        return jnp.sum(jnp.where(eye, row_values, 0), axis=1, keepdims=True)

    def parent_column(b):
        return column(PAR[pl.ds(b, 1), :])

    def gather_matrix(b, parents_col):
        path_row = PATH[pl.ds(b, 1), :]
        lane8 = lax.broadcasted_iota(jnp.int32, (1, 8), 1)
        last = jnp.sum(jnp.where(lane8 == accepts[b] - 1, path_row, 0), axis=1, keepdims=True)
        source = jnp.where(sub64[:, :1] == 0, last, parents_col)
        return jnp.where(source == lane64, 1.0, 0.0).astype(BF16)

    parents_col = parent_column(me)
    reach = jnp.where(eye | ((parents_col == lane64) & (sub64 > 0)), 1.0, 0.0)
    for _ in range(6):
        half = reach.astype(BF16)
        reach = jnp.minimum(dot(half, half), 1.0)
    depth = jnp.sum(reach, axis=1, keepdims=True) - 1.0
    length = lengths[me]
    angles = (length.astype(F32) + depth) * FREQ[...]
    cosine = jnp.cos(angles)
    sine = jnp.sin(angles)
    closed = jnp.maximum(depth.astype(jnp.int32), WIN - 1 - length)
    gather_own = gather_matrix(me, parents_col)
    hid_parts = []
    for q in range(4):
        EQ[q] = gather_matrix(2 * q + k, parent_column(2 * q + k))
        hid_parts.append(dot(EQ[q, rows(y, 16), :], H[pl.ds(64 * q, 64), own_cols]))
    hid_y = jnp.concatenate(hid_parts, axis=0)

    lane = lax.broadcasted_iota(jnp.int32, (64, 128), 1)
    front = lax.rem(lane, 64) < 32
    low = lane < 64

    def rotated(u):
        turned = jnp.where(front, -pltpu.roll(u, 96, 1), pltpu.roll(u, 32, 1))
        return u * cosine + turned * sine

    eye256 = lax.broadcasted_iota(jnp.int32, (256, 256), 0) == lax.broadcasted_iota(jnp.int32, (256, 256), 1)

    def as_row(col):
        return jnp.sum(jnp.where(eye256, col, jnp.zeros_like(col)), axis=0, keepdims=True)

    c_copy.wait()
    for c in late:
        c.wait()
    IG2[...] = 1.0 / (FG[...] * FG[...])
    token_cols = [column(TOK[pl.ds(2 * q + k, 1), :]) for q in range(4)]
    token_row = as_row(jnp.concatenate(token_cols, axis=0))

    for copy in first:
        copy.wait_recv()
    raw = PF[rows(x), :] + recv1[1].astype(F32) + recv1[2].astype(F32) + recv1[3].astype(F32)
    pair = raw[:, 512:640]
    fresh = jnp.where(low, rotated(pair), pair).astype(BF16)
    path_row = PATH[pl.ds(me, 1), :]
    path_col = jnp.sum(jnp.where(eye8, path_row, 0), axis=1, keepdims=True)
    lane8x64 = lax.broadcasted_iota(jnp.int32, (8, 64), 1)
    sub8x64 = lax.broadcasted_iota(jnp.int32, (8, 64), 0)
    chosen = jnp.where((path_col == lane8x64) & (sub8x64 < accepts[me]), 1.0, 0.0).astype(BF16)
    out_cache[...] = dot(chosen, fresh).astype(BF16)

    slot = lax.broadcasted_iota(jnp.int32, (256, WIN), 1)
    closed4 = jnp.concatenate([closed] * 4, axis=0)
    reach4 = jnp.concatenate([reach] * 4, axis=0) > 0.5
    spread = ([], [])
    for hc in range(2):
        stack = []
        for j in range(2):
            at = 256 * hc + 128 * j
            turned = rotated(raw[:, at : at + 128]).astype(BF16).astype(F32) * 0.125
            stack.append(jnp.where(low, turned, 0.0))
            stack.append(jnp.where(low, pltpu.roll(turned, 64, 1), 0.0))
        queries = jnp.concatenate(stack, axis=0).astype(BF16)
        scores = jnp.where(slot > closed4, dot_nt(queries, C[...]), -jnp.inf)
        scores_new = jnp.where(reach4, dot_nt(queries, fresh), -jnp.inf)
        top = jnp.maximum(jnp.max(scores, axis=1, keepdims=True), jnp.max(scores_new, axis=1, keepdims=True))
        w = jnp.exp(scores - top)
        w_new = jnp.exp(scores_new - top)
        total = jnp.sum(w, axis=1, keepdims=True) + jnp.sum(w_new, axis=1, keepdims=True)
        o = (dot(w.astype(BF16), C[...]) + dot(w_new.astype(BF16), fresh)) / total
        blocks = [
            jnp.where(low, pltpu.roll(o[128 * j : 128 * j + 64], 64, 1), o[128 * j + 64 : 128 * j + 128])
            for j in range(2)
        ]
        attended = jnp.concatenate(blocks, axis=1).astype(BF16)
        AS[hc] = dot(gather_own, attended).astype(BF16)
        for dx in FAR_FIRST:
            for dy in FAR_FIRST:
                if dx or dy:
                    to_y = ring(y, dy)
                    copy = remote(
                        AS.at[hc, rows(to_y, 16)], AR.at[hc, x, :, rows(y, 256)],
                        axs.at[hc, dx, dy], axr.at[hc, dx, dy], dev(ring(x, dx), k, to_y),
                    )
                    copy.start()
                    spread[hc].append(copy)
        AR[hc, x, :, rows(y, 256)] = AS[hc, rows(y, 16), :]

    wo_forwards = []
    for d in NEAR_FIRST:
        for hc in range(2):
            wo_gathers[hc, d].wait_recv()
            at = wo_piece(hc, ring(y, 4 - d))
            copy = remote(at, at, wps.at[hc, d], wpr.at[hc, d], partner)
            copy.start()
            wo_forwards.append(copy)
    for c in wo_copies:
        c.wait()
    for c in wo_swaps + wo_forwards:
        c.wait_recv()
    res = hid_y
    for hc in range(2):
        for copy in spread[hc]:
            copy.wait_recv()
        res = res + dot(AR[hc].reshape(64, 1024), WO[hc])
    def piece(h, xx, yy):
        return G.at[h, :, rows(yy, 16), rows(xx, 256)]

    def stage_one_copy(h, d):
        at = piece(h, x, y)
        where = dev(x, k, ring(y, d)) if h == 0 else dev(ring(x, d), k, y)
        return remote(at, at, gas.at[h, d], gar.at[h, d], where)

    def stage_two_copy(h, e, d):
        if h == 0:
            at = piece(0, x, ring(y, 4 - d))
            where = dev(ring(x, e), k, y)
        else:
            at = piece(1, ring(x, 4 - d), y)
            where = dev(x, k, ring(y, e))
        return remote(at, at, gbs.at[h, e, d], gbr.at[h, e, d], where)

    stage_one, stage_two = {}, {}
    for h in range(2):
        gain = FG[:, pl.ds(pl.multiple_of(512 * x + 256 * h, 256), 256)]
        part = (res[:, 256 * h : 256 * h + 256] * gain).astype(BF16)
        G[h, :, rows(y, 16), rows(x, 256)] = part.reshape(4, 16, 256)
        for d in NEAR_FIRST:
            stage_one[h, d] = stage_one_copy(h, d)
            stage_one[h, d].start()
    for h in range(2):
        for e in NEAR_FIRST:
            stage_two[h, e, 0] = stage_two_copy(h, e, 0)
            stage_two[h, e, 0].start()
    for d in NEAR_FIRST:
        for h in range(2):
            stage_one[h, d].wait_recv()
            for e in NEAR_FIRST:
                stage_two[h, e, d] = stage_two_copy(h, e, d)
                stage_two[h, e, d].start()

    for c in wh_copies:
        c.wait()
    for c in wh_swaps:
        c.wait_recv()

    def squares(h, xx):
        u = G[h, :, :, rows(xx, 256)].reshape(256, 256).astype(F32)
        scale = IG2[:, pl.ds(pl.multiple_of(512 * xx + 256 * h, 256), 256)]
        return jnp.sum(u * u * scale, axis=1, keepdims=True)

    sq = jnp.zeros((256, 1), F32)
    for e in (0,) + NEAR_FIRST:
        xx = ring(x, 4 - e)
        if e:
            for d in range(4):
                stage_two[0, e, d].wait_recv()
        sq = sq + squares(0, xx)
        cols = rows(xx, 256)
        rhs = G[0, :, :, cols].reshape(256, 256)

        def add_chunk(s, carry, rhs=rhs, cols=cols, begin=(e == 0)):
            term = dot_nt(WV[s, 0, :, cols], rhs)
            ACC[s] = term if begin else ACC[s] + term
            return carry

        lax.fori_loop(0, 2, add_chunk, 0)
    for e in NEAR_FIRST:
        for d in range(4):
            stage_two[1, e, d].wait_recv()
    for xx in range(4):
        sq = sq + squares(1, xx)
    inv = as_row(lax.rsqrt(sq * (1.0 / D) + EPS))

    def finish(s, top):
        t = (ACC[s] + dot_nt(WV[s, 1], G[1].reshape(256, 1024))) * inv
        ACC[s] = t
        return jnp.maximum(top, jnp.max(t, axis=0, keepdims=True))

    top = lax.fori_loop(0, 2, finish, jnp.full((1, 256), -jnp.inf, F32))
    vocab = lax.broadcasted_iota(jnp.int32, (VW, 256), 0)

    def totals(s, carry):
        total, pick = carry
        t = ACC[s]
        holder = jnp.where(s == 0, k, other)
        start = ((2 * x + holder) * 4 + y) * VW
        total = total + jnp.sum(jnp.exp(t - top), axis=0, keepdims=True)
        pick = pick + jnp.sum(jnp.where(vocab == token_row - start, t, 0.0), axis=0, keepdims=True)
        return total, pick

    zero = jnp.zeros((1, 256), F32)
    total, pick = lax.fori_loop(0, 2, totals, (zero, zero))
    def split(v):
        return [v[:, 0:128], v[:, 128:256]]

    ST[k, x, y] = jnp.concatenate(split(top) + split(total) + split(pick) + [jnp.zeros((2, 128), F32)], axis=0)
    third = []
    for i, (dx, dy, flip) in enumerate(everyone):
        at = ST.at[k, x, y]
        copy = remote(at, at, sts.at[i], str_.at[i], peers[i])
        copy.start()
        third.append(copy)

    first_of = lax.broadcasted_iota(jnp.int32, (8, 256), 0) * 64 == lax.broadcasted_iota(jnp.int32, (8, 256), 1)
    first_of = jnp.where(first_of, 1.0, 0.0)

    def last_rows(s):
        return lax.dot_general(
            first_of, ACC[s], (((1,), (1,)), ((), ())),
            precision=lax.Precision.HIGHEST, preferred_element_type=F32,
        )

    nx_send[...] = last_rows(1)
    nx = remote(nx_send, nx_recv, nxs, nxr, partner)
    nx.start()
    own_next = last_rows(0)

    nx.wait_recv()
    for copy in third:
        copy.wait_recv()
    lane1 = lax.broadcasted_iota(jnp.int32, (1, 64), 1)
    for plane in range(2):
        parts = [ST[plane, xx, yy] for xx in range(4) for yy in range(4)]
        tops = [p[0:2] for p in parts]
        m = functools.reduce(jnp.maximum, tops)
        whole = sum(p[2:4] * jnp.exp(t - m) for p, t in zip(parts, tops))
        log_total = m + jnp.log(whole)
        score = sum(p[4:6] for p in parts) - log_total
        for q in range(4):
            b = 2 * q + plane
            at = 64 * (q % 2)
            live = (lane1 > 0) & (lane1 < counts[b])
            out_node[pl.ds(b, 1), :] = jnp.where(live, score[q // 2 : q // 2 + 1, at : at + 64], 0.0)
            row = jnp.where(k == plane, own_next[q : q + 1], nx_recv[pl.ds(q, 1), :])
            out_next[pl.ds(b, 1), :] = row - log_total[q // 2 : q // 2 + 1, at : at + 1]

    for copy in swaps + list(wo_gathers.values()) + wo_forwards + first + spread[0] + spread[1]:
        copy.wait_send()
    for copy in list(stage_one.values()) + list(stage_two.values()) + third + [nx]:
        copy.wait_send()


def emit(node, following, cache_rows, out_node, out_next, out_cache):
    out_node[...] = node[...]
    out_next[...] = following[...]
    out_cache[...] = cache_rows[...]


def shards(
    hidden, attention_gain, query_weight, key_value_weight, output_weight, final_gain, head_weight,
    key_value_cache, parents, counts, lengths, tokens, accepted_path, accept_count,
):
    half = 32
    freq = 10000.0 ** (-np.arange(half, dtype=np.float64) / half)
    freq = jnp.asarray(np.tile(freq, 4)[None], F32)
    anywhere = pl.BlockSpec(memory_space=pl.ANY)
    scalars = pl.BlockSpec(memory_space=pltpu.SMEM)
    vmem = pl.BlockSpec(memory_space=pltpu.VMEM)
    dma = pltpu.SemaphoreType.DMA
    shapes = (
        jax.ShapeDtypeStruct((8, NODES), F32),
        jax.ShapeDtypeStruct((8, VW), F32),
        jax.ShapeDtypeStruct((8, 128), BF16),
    )
    results = pl.pallas_call(
        body,
        out_shape=shapes,
        in_specs=[anywhere] * 12 + [scalars] * 3,
        out_specs=(vmem, vmem, vmem),
        scratch_shapes=[
            pltpu.VMEM((256, D), BF16),
            pltpu.VMEM((1, D), F32),
            pltpu.VMEM((512, 640), BF16),
            pltpu.VMEM((2, 1024, 512), BF16),
            pltpu.VMEM((1, D), F32),
            pltpu.VMEM((2, 2, VW, 1024), BF16),
            pltpu.VMEM((WIN, 128), BF16),
            pltpu.VMEM((8, NODES), jnp.int32),
            pltpu.VMEM((8, NODES), jnp.int32),
            pltpu.VMEM((8, 8), jnp.int32),
            pltpu.VMEM((1, 128), F32),
            pltpu.VMEM((256, 640), F32),
            pltpu.VMEM((256, 512), BF16),
            pltpu.VMEM((4, 64, 640), BF16),
            pltpu.VMEM((4, 64, 640), BF16),
            pltpu.VMEM((4, 64, 64), BF16),
            pltpu.VMEM((2, 64, 256), BF16),
            pltpu.VMEM((2, 4, 16, 1024), BF16),
            pltpu.VMEM((2, 4, 64, 1024), BF16),
            pltpu.VMEM((2, VW, 256), F32),
            pltpu.VMEM((1, D), F32),
            pltpu.VMEM((2, 4, 4, 8, 128), F32),
            pltpu.VMEM((8, VW), F32),
            pltpu.VMEM((8, VW), F32),
            dma((24,)), dma((12,)), dma((12,)), dma((2, 4)), dma((2, 4)), dma((2, 4)), dma((2, 4)),
            dma((4,)), dma((4,)), dma((2, 4, 4)), dma((2, 4, 4)),
            dma((2, 4)), dma((2, 4)), dma((2, 4, 4)), dma((2, 4, 4)),
            dma((31,)), dma((31,)), dma(()), dma(()),
        ],
        compiler_params=pltpu.CompilerParams(
            collective_id=0, has_side_effects=True, vmem_limit_bytes=60 * 1024 * 1024
        ),
        name="verify",
    )(
        hidden,
        attention_gain.reshape(1, D),
        query_weight,
        key_value_weight.reshape(256, 128),
        output_weight,
        final_gain.reshape(1, D),
        head_weight.T,
        key_value_cache.reshape(WIN, 128),
        parents,
        tokens,
        accepted_path,
        freq,
        counts,
        lengths,
        accept_count,
    )
    node, following, cache_rows = pl.pallas_call(
        emit, out_shape=shapes, in_specs=[vmem] * 3, out_specs=(vmem,) * 3, name="emit"
    )(*results)
    return node, following, cache_rows.reshape(1, 8, 1, 128)


def solution(mesh):
    in_specs = (
        P("req", None),
        P(),
        P("row", "col"),
        P("row", "col", None),
        P("col", "row"),
        P(),
        P(None, ("row", "col")),
        P(("req", "row"), None, "col", None),
        P("req", None),
        P("req"),
        P("req"),
        P("req", None),
        P("req", None),
        P("req"),
    )
    out_specs = (P("req", None), P("req", ("row", "col")), P(("req", "row"), None, "col", None))
    return jax.shard_map(shards, mesh=mesh, in_specs=in_specs, out_specs=out_specs, check_vma=False)
```
